512 devices in a mesh: row: 32 (over z, x), col: 16 (over y, core).
Axes of the slice: x: 4, y: 8, z: 8, core: 2. Of those that a mesh axis runs over, the one named last changes fastest.
Arguments:
- rhs: bfloat16 [524288, 256], P(('row', 'col')), may hold values from -6 to 6
- order: int32 [512, 1024], P(('row', 'col')), may hold values from 0 to 1023, each once within a row
- leaf_inverse: bfloat16 [1024, 512, 512], P(('row', 'col')), may hold values from -1 to 2
- leaf_column_generator: bfloat16 [1024, 512, 256], P(('row', 'col')), may hold values from -0.25 to 0.25
- factor_up: bfloat16 [512, 9, 256, 256], P(('row', 'col')), may hold values from -1 to 1
- downward_coupling_factors: bfloat16 [512, 9, 256, 256], P(('row', 'col')), may hold values from -1 to 2
Outputs:
- solution: bfloat16 [524288, 256], P(('row', 'col'))
The draws below stay inside these ranges and needn't reach their ends.
All inputs are finite; a program needn't handle non-finite values.
Results may differ from the reference program's by a relative error of at most 0.015.
Values may be sent and summed in bfloat16 or wider, within the bound.
No kernel may reach another device: no remote copies, remote signals or barrier semaphores. Data moves between devices by JAX's collectives and lax.ppermute only.
A program may use at most 64 MiB of HBM per device.

```python
import math
import jax
import jax.numpy as jnp
import numpy as np
from jax import lax

R = 256
G = 256
LEAF = 512
LEAVES_DEV = 2
LEVELS = 9
BINS_DEV = 1024
BINS = 524288
LEAVES = 1024
N_ROW = 32
N_COL = 16


def draw_leaf_inverse(key, part):
    shape = (LEAVES_DEV * N_ROW * N_COL, LEAF, LEAF)
    noise = jnp.clip(jax.random.normal(jax.random.fold_in(key, 21), shape, jnp.float32), -4.0, 4.0)
    diagonal_block = jnp.ones(shape[:-1], jnp.float32)
    eye = jnp.eye(LEAF, dtype=jnp.float32)
    return (diagonal_block[..., None] * eye + 0.5 * noise / math.sqrt(LEAF)).astype(jnp.bfloat16)


def draw_factor_up(key, part):
    shape = (N_ROW * N_COL, LEVELS, R, R)
    noise = jnp.clip(jax.random.normal(jax.random.fold_in(key, 31), shape, jnp.float32), -4.0, 4.0)
    diagonal_block = jnp.full(shape[:-1], 0.6, jnp.float32)
    eye = jnp.eye(R, dtype=jnp.float32)
    return (diagonal_block[..., None] * eye + 0.37 * noise / math.sqrt(R)).astype(jnp.bfloat16)


def draw_downward_coupling_factors(key, part):
    shape = (N_ROW * N_COL, LEVELS, R, R)
    noise = jnp.clip(jax.random.normal(jax.random.fold_in(key, 41), shape, jnp.float32), -4.0, 4.0)
    diagonal_block = jnp.full(shape[:-1], 1.2, jnp.float32)
    eye = jnp.eye(R, dtype=jnp.float32)
    return (diagonal_block[..., None] * eye + 0.37 * noise / math.sqrt(R)).astype(jnp.bfloat16)


def shard_levels(stream_key, extent, cuts, smallest, largest):
    loudness = 1.0
    for dim, shards_of in cuts:
        steps = jax.random.uniform(jax.random.fold_in(jax.random.fold_in(stream_key, 6), dim), (shards_of,), jnp.float32, smallest / len(cuts), largest / len(cuts))
        loudness = loudness * jnp.repeat(jnp.exp(steps), extent[dim] // shards_of).reshape((-1,) + (1,) * (len(extent) - 1 - dim))
    return loudness


def gaussian(rng, dims, width, limit, shards=(), kind=jnp.bfloat16):
    gain = shard_levels(rng, dims, shards, -0.22, 0.18) if shards else 1.0
    result = jax.random.normal(rng, dims, jnp.float32) * width * gain
    return jnp.minimum(jnp.maximum(result, -limit), limit).astype(kind)


def setup_inputs(seed: int = 0) -> dict:
    key_list = jax.random.split(jax.random.key(seed), 7)
    rhs = gaussian(key_list[0], (BINS, G), 1.0, 6.0, ((0, 512),))
    order = jax.vmap(lambda own: jax.random.permutation(own, BINS_DEV))(jax.random.split(key_list[1], (N_ROW * N_COL))).reshape((N_ROW * N_COL, BINS_DEV)).astype(jnp.int32)
    leaf_inverse = draw_leaf_inverse(jax.random.fold_in(key_list[6], 71), 0)
    leaf_column_generator = gaussian(key_list[3], (LEAVES, LEAF, R), LEAF ** -0.5, 0.25, ((0, 512),))
    factor_up = draw_factor_up(jax.random.fold_in(key_list[6], 71), 0)
    downward_coupling_factors = draw_downward_coupling_factors(jax.random.fold_in(key_list[6], 71), 0)
    return dict(rhs=rhs, order=order, leaf_inverse=leaf_inverse, leaf_column_generator=leaf_column_generator, factor_up=factor_up, downward_coupling_factors=downward_coupling_factors)


def leaf_section(pieces):
    blocks, inverse, basis = pieces
    eliminated_rows = jnp.einsum('jab,jbg->jag', inverse.astype(jnp.float32), blocks.astype(jnp.float32))
    rounded = lax.optimization_barrier(eliminated_rows.astype(jnp.bfloat16)).astype(jnp.float32)
    solve_state = jnp.einsum('dmq,dms->qs', basis.astype(jnp.float32), rounded)
    return eliminated_rows, solve_state


def finish_section(pieces):
    eliminated_rows, top, inverse, basis, positions = pieces
    top_half = lax.optimization_barrier(top.astype(jnp.bfloat16)).astype(jnp.float32)
    back = jnp.einsum('jar,rg->jag', basis.astype(jnp.float32), top_half)
    back_half = lax.optimization_barrier(back.astype(jnp.bfloat16)).astype(jnp.float32)
    solved = eliminated_rows - jnp.einsum('jab,jbg->jag', inverse.astype(jnp.float32), back_half)
    flat = solved.reshape(BINS_DEV, G).astype(jnp.bfloat16)
    placed = jnp.zeros((BINS_DEV, G), jnp.bfloat16)
    return placed.at[positions].set(flat)


def reference(rhs, order, leaf_inverse, leaf_column_generator, factor_up, downward_coupling_factors):
    devices = N_ROW * N_COL
    grouped = rhs.reshape(devices, BINS_DEV, G)
    ordered = jnp.take_along_axis(grouped, order[:, :, None], axis=1)
    blocks = ordered.reshape(devices, LEAVES_DEV, LEAF, G)
    inverse = leaf_inverse.reshape(devices, LEAVES_DEV, LEAF, LEAF)
    basis = leaf_column_generator.reshape(devices, LEAVES_DEV, LEAF, R)
    eliminated_rows, solve_state = lax.map(leaf_section, (blocks, inverse, basis))
    saved = []
    for level in range(LEVELS):
        partner = np.arange(devices) ^ (1 << level)
        saved.append(solve_state)
        rounded = lax.optimization_barrier(solve_state.astype(jnp.bfloat16)).astype(jnp.float32)
        term = jnp.einsum('dij,djg->dig', factor_up[:, level].astype(jnp.float32), rounded)
        term_half = lax.optimization_barrier(term.astype(jnp.bfloat16)).astype(jnp.float32)
        solve_state = term_half + term_half[partner]
    top = solve_state
    for level in reversed(range(LEVELS)):
        partner = np.arange(devices) ^ (1 << level)
        rounded = lax.optimization_barrier(top.astype(jnp.bfloat16)).astype(jnp.float32)
        own = jnp.einsum('dji,djg->dig', factor_up[:, level].astype(jnp.float32), rounded)
        sent = jnp.einsum('dij,djg->dig', downward_coupling_factors[:, level].astype(jnp.float32), rounded)
        sent_half = lax.optimization_barrier(sent.astype(jnp.bfloat16)).astype(jnp.float32)
        top = saved[level] + 0.5 * (sent_half[partner] - own)
    placed = lax.map(finish_section, (eliminated_rows, top, inverse, basis, order))
    return placed.reshape(BINS, G)
```

```python
import jax
import jax.numpy as jnp
from jax import lax
from jax.sharding import PartitionSpec as P


def pair_groups(size, bit):
    step = 1 << bit
    return [[i, i ^ step] for i in range(size) if not i & step]


def axis_of(level, col_bits):
    return ("col", level) if level < col_bits else ("row", level - col_bits)


def both(value, level, col_bits):
    axis, bit = axis_of(level, col_bits)
    groups = pair_groups(lax.axis_size(axis), bit)
    return lax.all_gather(value, axis, axis=0, tiled=False, axis_index_groups=groups)


def partner_part(pair, level, col_bits):
    axis, bit = axis_of(level, col_bits)
    high = (lax.axis_index(axis) >> bit) & 1
    return jnp.where(high == 1, pair[0], pair[1])


def times(kernel_matrix, value):
    return jnp.dot(kernel_matrix, value, preferred_element_type=jnp.float32)


def times_transposed(kernel_matrix, value):
    return jnp.einsum("ji,jg->ig", kernel_matrix, value, preferred_element_type=jnp.float32)


def on_device(
    rhs, order, leaf_inverse, leaf_column_generator, factor_up, downward_coupling_factors
):
    positions = order[0]
    leaves = leaf_inverse.shape[0]
    leaf = leaf_inverse.shape[1]
    genes = rhs.shape[1]
    ordered = jnp.take(rhs, positions, axis=0)
    blocks = ordered.reshape(leaves, leaf, genes)
    eliminated_rows = jnp.einsum(
        "jab,jbg->jag", leaf_inverse, blocks, preferred_element_type=jnp.float32
    )
    elimination_portion = eliminated_rows.astype(jnp.bfloat16)
    solve_state = jnp.einsum(
        "dmq,dms->qs",
        leaf_column_generator,
        elimination_portion,
        preferred_element_type=jnp.float32,
    )
    up_mats = factor_up[0]
    down_mats = downward_coupling_factors[0]
    levels = up_mats.shape[0]
    last = levels - 1
    col_bits = lax.axis_size("col").bit_length() - 1
    saved = []
    for level in range(levels):
        saved.append(solve_state)
        term = times(up_mats[level], solve_state.astype(jnp.bfloat16)).astype(jnp.bfloat16)
        if level == last:
            pair = both(jnp.stack([term, down_mats[level]]), level, col_bits)
            terms, coupling = pair[:, 0], pair[:, 1]
        else:
            terms = both(term, level, col_bits)
        solve_state = terms[0].astype(jnp.float32) + terms[1].astype(jnp.float32)
    top = solve_state
    for level in reversed(range(levels)):
        rounded = top.astype(jnp.bfloat16)
        own = times_transposed(up_mats[level], rounded)
        if level == last:
            coupled = times(partner_part(coupling, level, col_bits), rounded).astype(jnp.bfloat16)
        else:
            sent = times(down_mats[level], rounded).astype(jnp.bfloat16)
            coupled = partner_part(both(sent, level, col_bits), level, col_bits)
        top = saved[level] + 0.5 * (coupled.astype(jnp.float32) - own)
    top_half = top.astype(jnp.bfloat16)
    back = jnp.einsum(
        "jar,rg->jag", leaf_column_generator, top_half, preferred_element_type=jnp.float32
    ).astype(jnp.bfloat16)
    solved = eliminated_rows - jnp.einsum(
        "jab,jbg->jag", leaf_inverse, back, preferred_element_type=jnp.float32
    )
    flat = solved.reshape(leaves * leaf, genes).astype(jnp.bfloat16)
    placed = jnp.zeros((leaves * leaf, genes), jnp.bfloat16)
    return placed.at[positions].set(flat)


def solution(mesh):
    in_specs = (
        P(("row", "col"), None),
        P(("row", "col"), None),
        P(("row", "col"), None, None),
        P(("row", "col"), None, None),
        P(("row", "col"), None, None, None),
        P(("row", "col"), None, None, None),
    )
    out_specs = P(("row", "col"), None)
    return jax.shard_map(
        on_device, mesh=mesh, in_specs=in_specs, out_specs=out_specs, check_vma=False
    )
```

```python
import functools

import functools

import jax
import jax.numpy as jnp
from jax import lax
from jax.experimental import pallas as pl
from jax.experimental.pallas import tpu as pltpu
from jax.sharding import PartitionSpec as P

BF16 = jnp.bfloat16
F32 = jnp.float32
MIB = 1 << 20


def pair_groups(size, bit):
    step = 1 << bit
    return [[i, i ^ step] for i in range(size) if not i & step]


def axis_of(level, col_bits):
    return ("col", level) if level < col_bits else ("row", level - col_bits)


def both(value, level, col_bits):
    axis, bit = axis_of(level, col_bits)
    groups = pair_groups(lax.axis_size(axis), bit)
    return lax.all_gather(value, axis, axis=0, tiled=False, axis_index_groups=groups)


def partner_slot(level, col_bits):
    axis, bit = axis_of(level, col_bits)
    return 1 - lax.rem(lax.div(lax.axis_index(axis), 1 << bit), 2)


def times(a, b):
    return jnp.dot(a, b, preferred_element_type=F32)


def times_transposed(a, b):
    return lax.dot_general(a, b, (((0,), (0,)), ((), ())), preferred_element_type=F32)


def pair_sum(pair_ref):
    return pair_ref[0].astype(F32) + pair_ref[1].astype(F32)


def call(kernel, outs, n_in, limit):
    vmem = [pl.BlockSpec(memory_space=pltpu.VMEM)] * n_in
    return pl.pallas_call(
        kernel,
        out_shape=[jax.ShapeDtypeStruct(shape, dtype) for shape, dtype in outs],
        in_specs=vmem,
        out_specs=[pl.BlockSpec(memory_space=pltpu.VMEM)] * len(outs),
        compiler_params=pltpu.CompilerParams(vmem_limit_bytes=limit),
    )


def leaf_kernel(order_ref, rhs_ref, inverse_ref, basis_ref, up_ref, rows_ref, state_ref, term_ref):
    rows = rhs_ref.shape[0]
    leaves, leaf = inverse_ref.shape[:2]
    across = jnp.broadcast_to(order_ref[...], (128, rows)).T
    lane = lax.broadcasted_iota(jnp.int32, (rows, 128), 1)
    pick = jnp.concatenate(
        [jnp.where(across == lane + 128 * b, 1.0, 0.0).astype(BF16) for b in range(rows // 128)],
        axis=1,
    )
    ordered = times(pick, rhs_ref[...]).astype(BF16)
    state = None
    for j in range(leaves):
        block = times(inverse_ref[j], ordered[j * leaf : (j + 1) * leaf])
        rows_ref[j] = block
        part = times_transposed(basis_ref[j], block.astype(BF16))
        state = part if state is None else state + part
    state_ref[...] = state
    term_ref[...] = times(up_ref[0, 0], state.astype(BF16)).astype(BF16)


def up_kernel(level, pair_ref, up_ref, term_ref):
    term_ref[...] = times(up_ref[0, level], pair_sum(pair_ref).astype(BF16)).astype(BF16)


def last_up_kernel(level, pair_ref, up_ref, down_ref, out_ref):
    out_ref[0] = times(up_ref[0, level], pair_sum(pair_ref).astype(BF16)).astype(BF16)
    out_ref[1] = down_ref[0, level]


def top_kernel(level, col_bits, pair_ref, saved_ref, up_ref, down_ref, y_ref, sent_ref):
    y = (pair_ref[0, 0].astype(F32) + pair_ref[1, 0].astype(F32)).astype(BF16)
    coupled = times(pair_ref[partner_slot(level, col_bits), 1], y).astype(BF16).astype(F32)
    top = pair_sum(saved_ref) + 0.5 * (coupled - times_transposed(up_ref[0, level], y))
    y_ref[...] = top.astype(BF16)
    sent_ref[...] = times(down_ref[0, level - 1], top.astype(BF16)).astype(BF16)


def down_kernel(level, col_bits, pair_ref, saved_ref, above_ref, up_ref, down_ref, y_ref, sent_ref):
    coupled = pair_ref[partner_slot(level, col_bits)].astype(F32)
    top = pair_sum(saved_ref) + 0.5 * (coupled - times_transposed(up_ref[0, level], above_ref[...]))
    y_ref[...] = top.astype(BF16)
    sent_ref[...] = times(down_ref[0, level - 1], top.astype(BF16)).astype(BF16)


def last_kernel(
    col_bits, order_ref, pair_ref, state_ref, above_ref, up_ref, inverse_ref, basis_ref, rows_ref, out_ref
):
    rows = out_ref.shape[0]
    leaves = inverse_ref.shape[0]
    coupled = pair_ref[partner_slot(0, col_bits)].astype(F32)
    top = state_ref[...] + 0.5 * (coupled - times_transposed(up_ref[0, 0], above_ref[...]))
    top_half = top.astype(BF16)
    solved = []
    for j in range(leaves):
        back = times(basis_ref[j], top_half).astype(BF16)
        solved.append((rows_ref[j] - times(inverse_ref[j], back)).astype(BF16))
    place = lax.broadcasted_iota(jnp.int32, (rows, rows), 0) == order_ref[...]
    pick = jnp.where(place, 1.0, 0.0).astype(BF16)
    out_ref[...] = times(pick, jnp.concatenate(solved, axis=0)).astype(BF16)


def on_device(
    rhs, order, leaf_inverse, leaf_column_generator, factor_up, downward_coupling_factors
):
    leaves, leaf = leaf_inverse.shape[:2]
    rank = leaf_column_generator.shape[2]
    genes = rhs.shape[1]
    levels = factor_up.shape[1]
    last = levels - 1
    col_bits = lax.axis_size("col").bit_length() - 1
    up, down = factor_up, downward_coupling_factors
    small = (rank, genes)
    steps = [(small, BF16), (small, BF16)]

    rows, state, term = call(
        leaf_kernel, [((leaves, leaf, genes), F32), (small, F32), (small, BF16)], 5, 24 * MIB
    )(order, rhs, leaf_inverse, leaf_column_generator, up)
    pairs = [both(term, 0, col_bits)]
    for level in range(1, last):
        (term,) = call(functools.partial(up_kernel, level), [(small, BF16)], 2, 4 * MIB)(pairs[-1], up)
        pairs.append(both(term, level, col_bits))
    (packed,) = call(functools.partial(last_up_kernel, last), [((2,) + small, BF16)], 3, 4 * MIB)(pairs[-1], up, down)
    y, sent = call(functools.partial(top_kernel, last, col_bits), steps, 4, 6 * MIB)(
        both(packed, last, col_bits), pairs[last - 1], up, down
    )
    for level in range(last - 1, 0, -1):
        y, sent = call(functools.partial(down_kernel, level, col_bits), steps, 5, 6 * MIB)(
            both(sent, level, col_bits), pairs[level - 1], y, up, down
        )
    (solved,) = call(functools.partial(last_kernel, col_bits), [(rhs.shape, BF16)], 8, 24 * MIB)(
        order, both(sent, 0, col_bits), state, y, up, leaf_inverse, leaf_column_generator, rows
    )
    return solved


def solution(mesh):
    in_specs = (
        P(("row", "col"), None),
        P(("row", "col"), None),
        P(("row", "col"), None, None),
        P(("row", "col"), None, None),
        P(("row", "col"), None, None, None),
        P(("row", "col"), None, None, None),
    )
    out_specs = P(("row", "col"), None)
    return jax.shard_map(
        on_device, mesh=mesh, in_specs=in_specs, out_specs=out_specs, check_vma=False
    )
```

```python
import functools

import functools

import jax
import jax.numpy as jnp
from jax import lax
from jax.experimental import pallas as pl
from jax.experimental.pallas import tpu as pltpu
from jax.sharding import PartitionSpec as P

BF16 = jnp.bfloat16
F32 = jnp.float32
MIB = 1 << 20


def pair_groups(size, bit):
    step = 1 << bit
    return [[i, i ^ step] for i in range(size) if not i & step]


def axis_of(level, col_bits):
    return ("col", level) if level < col_bits else ("row", level - col_bits)


def both(value, level, col_bits):
    axis, bit = axis_of(level, col_bits)
    groups = pair_groups(lax.axis_size(axis), bit)
    return lax.all_gather(value, axis, axis=0, tiled=False, axis_index_groups=groups)


def partner_slot(level, col_bits):
    axis, bit = axis_of(level, col_bits)
    return 1 - lax.rem(lax.div(lax.axis_index(axis), 1 << bit), 2)


def times(a, b):
    return jnp.dot(a, b, preferred_element_type=F32)


def times_transposed(a, b):
    return lax.dot_general(a, b, (((0,), (0,)), ((), ())), preferred_element_type=F32)


def pair_sum(pair_ref):
    return pair_ref[0].astype(F32) + pair_ref[1].astype(F32)


def call(kernel, outs, n_in, limit):
    vmem = [pl.BlockSpec(memory_space=pltpu.VMEM)] * n_in
    return pl.pallas_call(
        kernel,
        out_shape=[jax.ShapeDtypeStruct(shape, dtype) for shape, dtype in outs],
        in_specs=vmem,
        out_specs=[pl.BlockSpec(memory_space=pltpu.VMEM)] * len(outs),
        compiler_params=pltpu.CompilerParams(vmem_limit_bytes=limit),
    )


def leaf_kernel(
    order_hbm, rhs_hbm, inverse_hbm, basis_hbm, up_hbm, rows_ref, state_ref, term_ref,
    order_ref, rhs_ref, inverse_ref, basis_ref, up_ref, sems,
):
    rows = rhs_ref.shape[0]
    leaves, leaf = inverse_ref.shape[:2]
    moves = [
        pltpu.make_async_copy(src, dst, sems.at[k])
        for k, (src, dst) in enumerate(
            [
                (order_hbm, order_ref),
                (rhs_hbm, rhs_ref),
                (inverse_hbm, inverse_ref),
                (basis_hbm, basis_ref),
                (up_hbm.at[0, 0], up_ref),
            ]
        )
    ]
    for move in moves:
        move.start()
    moves[0].wait()
    across = jnp.broadcast_to(order_ref[...], (128, rows)).T
    lane = lax.broadcasted_iota(jnp.int32, (rows, 128), 1)
    pick = jnp.concatenate(
        [jnp.where(across == lane + 128 * b, 1.0, 0.0).astype(BF16) for b in range(rows // 128)],
        axis=1,
    )
    moves[1].wait()
    ordered = times(pick, rhs_ref[...]).astype(BF16)
    moves[2].wait()
    moves[3].wait()
    state = None
    for j in range(leaves):
        block = times(inverse_ref[j], ordered[j * leaf : (j + 1) * leaf])
        rows_ref[j] = block
        part = times_transposed(basis_ref[j], block.astype(BF16))
        state = part if state is None else state + part
    state_ref[...] = state
    moves[4].wait()
    term_ref[...] = times(up_ref[...], state.astype(BF16)).astype(BF16)


def up_kernel(level, pair_ref, up_ref, term_ref):
    term_ref[...] = times(up_ref[0, level], pair_sum(pair_ref).astype(BF16)).astype(BF16)


def last_up_kernel(level, pair_ref, up_ref, down_ref, out_ref):
    out_ref[0] = times(up_ref[0, level], pair_sum(pair_ref).astype(BF16)).astype(BF16)
    out_ref[1] = down_ref[0, level]


def top_kernel(level, col_bits, pair_ref, saved_ref, up_ref, down_ref, y_ref, sent_ref):
    y = (pair_ref[0, 0].astype(F32) + pair_ref[1, 0].astype(F32)).astype(BF16)
    coupled = times(pair_ref[partner_slot(level, col_bits), 1], y).astype(BF16).astype(F32)
    top = pair_sum(saved_ref) + 0.5 * (coupled - times_transposed(up_ref[0, level], y))
    y_ref[...] = top.astype(BF16)
    sent_ref[...] = times(down_ref[0, level - 1], top.astype(BF16)).astype(BF16)


def down_kernel(level, col_bits, pair_ref, saved_ref, above_ref, up_ref, down_ref, y_ref, sent_ref):
    coupled = pair_ref[partner_slot(level, col_bits)].astype(F32)
    top = pair_sum(saved_ref) + 0.5 * (coupled - times_transposed(up_ref[0, level], above_ref[...]))
    y_ref[...] = top.astype(BF16)
    sent_ref[...] = times(down_ref[0, level - 1], top.astype(BF16)).astype(BF16)


def last_kernel(
    col_bits, order_ref, pair_ref, state_ref, above_ref, up_ref, inverse_ref, basis_ref, rows_ref, out_ref
):
    rows = out_ref.shape[0]
    leaves = inverse_ref.shape[0]
    coupled = pair_ref[partner_slot(0, col_bits)].astype(F32)
    top = state_ref[...] + 0.5 * (coupled - times_transposed(up_ref[0, 0], above_ref[...]))
    top_half = top.astype(BF16)
    solved = []
    for j in range(leaves):
        back = times(basis_ref[j], top_half).astype(BF16)
        solved.append((rows_ref[j] - times(inverse_ref[j], back)).astype(BF16))
    place = lax.broadcasted_iota(jnp.int32, (rows, rows), 0) == order_ref[...]
    pick = jnp.where(place, 1.0, 0.0).astype(BF16)
    out_ref[...] = times(pick, jnp.concatenate(solved, axis=0)).astype(BF16)


def on_device(
    rhs, order, leaf_inverse, leaf_column_generator, factor_up, downward_coupling_factors
):
    leaves, leaf = leaf_inverse.shape[:2]
    rank = leaf_column_generator.shape[2]
    genes = rhs.shape[1]
    levels = factor_up.shape[1]
    last = levels - 1
    col_bits = lax.axis_size("col").bit_length() - 1
    up, down = factor_up, downward_coupling_factors
    small = (rank, genes)
    steps = [(small, BF16), (small, BF16)]

    rows, state, term = pl.pallas_call(
        leaf_kernel,
        out_shape=[
            jax.ShapeDtypeStruct((leaves, leaf, genes), F32),
            jax.ShapeDtypeStruct(small, F32),
            jax.ShapeDtypeStruct(small, BF16),
        ],
        in_specs=[pl.BlockSpec(memory_space=pltpu.HBM)] * 5,
        out_specs=[pl.BlockSpec(memory_space=pltpu.VMEM)] * 3,
        scratch_shapes=[
            pltpu.VMEM(order.shape, order.dtype),
            pltpu.VMEM(rhs.shape, BF16),
            pltpu.VMEM(leaf_inverse.shape, BF16),
            pltpu.VMEM(leaf_column_generator.shape, BF16),
            pltpu.VMEM(factor_up.shape[2:], BF16),
            pltpu.SemaphoreType.DMA((5,)),
        ],
        compiler_params=pltpu.CompilerParams(vmem_limit_bytes=56 * MIB),
    )(order, rhs, leaf_inverse, leaf_column_generator, up)
    pairs = [both(term, 0, col_bits)]
    for level in range(1, last):
        (term,) = call(functools.partial(up_kernel, level), [(small, BF16)], 2, 4 * MIB)(pairs[-1], up)
        pairs.append(both(term, level, col_bits))
    (packed,) = call(functools.partial(last_up_kernel, last), [((2,) + small, BF16)], 3, 4 * MIB)(pairs[-1], up, down)
    y, sent = call(functools.partial(top_kernel, last, col_bits), steps, 4, 6 * MIB)(
        both(packed, last, col_bits), pairs[last - 1], up, down
    )
    for level in range(last - 1, 0, -1):
        y, sent = call(functools.partial(down_kernel, level, col_bits), steps, 5, 6 * MIB)(
            both(sent, level, col_bits), pairs[level - 1], y, up, down
        )
    (solved,) = call(functools.partial(last_kernel, col_bits), [(rhs.shape, BF16)], 8, 24 * MIB)(
        order, both(sent, 0, col_bits), state, y, up, leaf_inverse, leaf_column_generator, rows
    )
    return solved


def solution(mesh):
    in_specs = (
        P(("row", "col"), None),
        P(("row", "col"), None),
        P(("row", "col"), None, None),
        P(("row", "col"), None, None),
        P(("row", "col"), None, None, None),
        P(("row", "col"), None, None, None),
    )
    out_specs = P(("row", "col"), None)
    return jax.shard_map(
        on_device, mesh=mesh, in_specs=in_specs, out_specs=out_specs, check_vma=False
    )
```

```python
import functools

import functools

import jax
import jax.numpy as jnp
from jax import lax
from jax.experimental import pallas as pl
from jax.experimental.pallas import tpu as pltpu
from jax.sharding import PartitionSpec as P


BF16 = jnp.bfloat16
F32 = jnp.float32
MIB = 1 << 20


def pair_groups(size, bit):
    step = 1 << bit
    return [[i, i ^ step] for i in range(size) if not i & step]


def axis_of(level, col_bits):
    return ("col", level) if level < col_bits else ("row", level - col_bits)


def both(value, level, col_bits):
    axis, bit = axis_of(level, col_bits)
    groups = pair_groups(lax.axis_size(axis), bit)
    return lax.all_gather(value, axis, axis=0, tiled=False, axis_index_groups=groups)


def among_four(value, level, col_bits):
    axis, bit = axis_of(level, col_bits)
    step, size = 1 << bit, lax.axis_size(axis)
    groups = [[i + step * k for k in range(4)] for i in range(size) if not i & (3 * step)]
    return lax.all_to_all(value, axis, 0, 0, axis_index_groups=groups)


def partner_slot(level, col_bits):
    axis, bit = axis_of(level, col_bits)
    return 1 - lax.rem(lax.div(lax.axis_index(axis), 1 << bit), 2)


def times(a, b):
    return jnp.dot(a, b, preferred_element_type=F32)


def times_transposed(a, b):
    return lax.dot_general(a, b, (((0,), (0,)), ((), ())), preferred_element_type=F32)


def pair_sum(pair_ref):
    return pair_ref[0].astype(F32) + pair_ref[1].astype(F32)


def call(kernel, outs, n_in, limit):
    vmem = [pl.BlockSpec(memory_space=pltpu.VMEM)] * n_in
    return pl.pallas_call(
        kernel,
        out_shape=[jax.ShapeDtypeStruct(shape, dtype) for shape, dtype in outs],
        in_specs=vmem,
        out_specs=[pl.BlockSpec(memory_space=pltpu.VMEM)] * len(outs),
        compiler_params=pltpu.CompilerParams(vmem_limit_bytes=limit),
    )


def leaf_kernel(
    order_hbm, rhs_hbm, inverse_hbm, basis_hbm, up_hbm, down_hbm, rows_ref, state_ref, term_ref, share_hbm,
    order_ref, rhs_ref, inverse_ref, basis_ref, up_ref, share_ref, sems, share_sems,
):
    last = up_hbm.shape[1] - 1
    rows = rhs_ref.shape[0]
    leaves, leaf = inverse_ref.shape[:2]
    moves = [
        pltpu.make_async_copy(src, dst, sems.at[k])
        for k, (src, dst) in enumerate(
            [
                (order_hbm, order_ref),
                (rhs_hbm, rhs_ref),
                (inverse_hbm, inverse_ref),
                (basis_hbm, basis_ref),
                (up_hbm.at[0, 0], up_ref),
                (up_hbm.at[0, last], share_ref.at[0]),
                (down_hbm.at[0, last], share_ref.at[1]),
                (down_hbm.at[0, last - 1], share_ref.at[2]),
            ]
        )
    ]
    for move in moves:
        move.start()
    moves[0].wait()
    across = jnp.broadcast_to(order_ref[...], (128, rows)).T
    lane = lax.broadcasted_iota(jnp.int32, (rows, 128), 1)
    pick = jnp.concatenate(
        [jnp.where(across == lane + 128 * b, 1.0, 0.0).astype(BF16) for b in range(rows // 128)],
        axis=1,
    )
    moves[1].wait()
    for move in moves[5:]:
        move.wait()
    spread = [
        pltpu.make_async_copy(share_ref, share_hbm.at[k], share_sems.at[k])
        for k in range(share_hbm.shape[0])
    ]
    for move in spread:
        move.start()
    ordered = times(pick, rhs_ref[...]).astype(BF16)
    moves[2].wait()
    moves[3].wait()
    state = None
    for j in range(leaves):
        block = times(inverse_ref[j], ordered[j * leaf : (j + 1) * leaf])
        rows_ref[j] = block
        part = times_transposed(basis_ref[j], block.astype(BF16))
        state = part if state is None else state + part
    state_ref[...] = state
    moves[4].wait()
    term_ref[...] = times(up_ref[...], state.astype(BF16)).astype(BF16)
    for move in spread:
        move.wait()


def up_kernel(level, pair_ref, up_ref, term_ref):
    term_ref[...] = times(up_ref[0, level], pair_sum(pair_ref).astype(BF16)).astype(BF16)


def spread_kernel(level, pair_ref, up_ref, out_ref):
    term = times(up_ref[0, level], pair_sum(pair_ref).astype(BF16)).astype(BF16)
    for k in range(out_ref.shape[0]):
        out_ref[k] = term


def top_kernel(low, col_bits, terms_ref, share_ref, saved_ref, up_ref, down_ref, y_ref, sent_ref):
    axis, bit = axis_of(low, col_bits)
    me = lax.rem(lax.div(lax.axis_index(axis), 1 << bit), 4)
    flip = 1 - 2 * lax.rem(me, 2)
    across = 2 - 4 * lax.div(me, 2)
    a, b, c, d = me, me + flip, me + across, me + flip + across

    def rounded(x):
        return x.astype(BF16)

    def elim(member, value):
        return rounded(times(share_ref[member, 0], value)).astype(F32)

    def above(member, other, state, value):
        coupled = rounded(times(share_ref[other, 1], value)).astype(F32)
        return state + 0.5 * (coupled - times_transposed(share_ref[member, 0], value))

    state = terms_ref[a].astype(F32) + terms_ref[b].astype(F32)
    far = terms_ref[c].astype(F32) + terms_ref[d].astype(F32)
    state_half, far_half = rounded(state), rounded(far)
    y_mine = rounded(elim(a, state_half) + elim(c, far_half))
    y_near = rounded(elim(b, state_half) + elim(d, far_half))
    top_mine = rounded(above(a, c, state, y_mine))
    top_near = rounded(above(b, d, state, y_near))
    coupled = rounded(times(share_ref[b, 2], top_near)).astype(F32)
    top = rounded(pair_sum(saved_ref) + 0.5 * (coupled - times_transposed(up_ref[0, low], top_mine)))
    y_ref[...] = top
    sent_ref[...] = rounded(times(down_ref[0, low - 1], top))


def down_kernel(level, col_bits, pair_ref, saved_ref, above_ref, up_ref, down_ref, y_ref, sent_ref):
    coupled = pair_ref[partner_slot(level, col_bits)].astype(F32)
    top = pair_sum(saved_ref) + 0.5 * (coupled - times_transposed(up_ref[0, level], above_ref[...]))
    y_ref[...] = top.astype(BF16)
    sent_ref[...] = times(down_ref[0, level - 1], top.astype(BF16)).astype(BF16)


def last_kernel(
    col_bits, order_ref, pair_ref, state_ref, above_ref, up_ref, inverse_ref, basis_ref, rows_ref, out_ref
):
    rows = out_ref.shape[0]
    leaves = inverse_ref.shape[0]
    coupled = pair_ref[partner_slot(0, col_bits)].astype(F32)
    top = state_ref[...] + 0.5 * (coupled - times_transposed(up_ref[0, 0], above_ref[...]))
    top_half = top.astype(BF16)
    solved = []
    for j in range(leaves):
        back = times(basis_ref[j], top_half).astype(BF16)
        solved.append((rows_ref[j] - times(inverse_ref[j], back)).astype(BF16))
    place = lax.broadcasted_iota(jnp.int32, (rows, rows), 0) == order_ref[...]
    pick = jnp.where(place, 1.0, 0.0).astype(BF16)
    out_ref[...] = times(pick, jnp.concatenate(solved, axis=0)).astype(BF16)


def on_device(
    rhs, order, leaf_inverse, leaf_column_generator, factor_up, downward_coupling_factors
):
    leaves, leaf = leaf_inverse.shape[:2]
    rank = leaf_column_generator.shape[2]
    genes = rhs.shape[1]
    levels = factor_up.shape[1]
    last = levels - 1
    col_bits = lax.axis_size("col").bit_length() - 1
    up, down = factor_up, downward_coupling_factors
    small = (rank, genes)
    steps = [(small, BF16), (small, BF16)]

    rows, state, term, share = pl.pallas_call(
        leaf_kernel,
        out_shape=[
            jax.ShapeDtypeStruct((leaves, leaf, genes), F32),
            jax.ShapeDtypeStruct(small, F32),
            jax.ShapeDtypeStruct(small, BF16),
            jax.ShapeDtypeStruct((4, 3) + factor_up.shape[2:], BF16),
        ],
        in_specs=[pl.BlockSpec(memory_space=pltpu.HBM)] * 6,
        out_specs=[pl.BlockSpec(memory_space=pltpu.VMEM)] * 3 + [pl.BlockSpec(memory_space=pltpu.HBM)],
        scratch_shapes=[
            pltpu.VMEM(order.shape, order.dtype),
            pltpu.VMEM(rhs.shape, BF16),
            pltpu.VMEM(leaf_inverse.shape, BF16),
            pltpu.VMEM(leaf_column_generator.shape, BF16),
            pltpu.VMEM(factor_up.shape[2:], BF16),
            pltpu.VMEM((3,) + factor_up.shape[2:], BF16),
            pltpu.SemaphoreType.DMA((8,)),
            pltpu.SemaphoreType.DMA((4,)),
        ],
        compiler_params=pltpu.CompilerParams(vmem_limit_bytes=56 * MIB),
    )(order, rhs, leaf_inverse, leaf_column_generator, up, down)
    pairs = [both(term, 0, col_bits)]
    low = last - 1
    shared = among_four(share, low, col_bits)
    for level in range(1, low):
        (term,) = call(functools.partial(up_kernel, level), [(small, BF16)], 2, 4 * MIB)(pairs[-1], up)
        if level == low - 1:
            term, shared = lax.optimization_barrier((term, shared))
        pairs.append(both(term, level, col_bits))
    (terms,) = call(functools.partial(spread_kernel, low), [((4,) + small, BF16)], 2, 4 * MIB)(pairs[-1], up)
    y, sent = call(functools.partial(top_kernel, low, col_bits), steps, 5, 8 * MIB)(
        among_four(terms, low, col_bits), shared, pairs[-1], up, down
    )
    for level in range(low - 1, 0, -1):
        y, sent = call(functools.partial(down_kernel, level, col_bits), steps, 5, 6 * MIB)(
            both(sent, level, col_bits), pairs[level - 1], y, up, down
        )
    (solved,) = call(functools.partial(last_kernel, col_bits), [(rhs.shape, BF16)], 8, 24 * MIB)(
        order, both(sent, 0, col_bits), state, y, up, leaf_inverse, leaf_column_generator, rows
    )
    return solved


def solution(mesh):
    in_specs = (
        P(("row", "col"), None),
        P(("row", "col"), None),
        P(("row", "col"), None, None),
        P(("row", "col"), None, None),
        P(("row", "col"), None, None, None),
        P(("row", "col"), None, None, None),
    )
    out_specs = P(("row", "col"), None)

    return jax.shard_map(on_device, mesh=mesh, in_specs=in_specs, out_specs=out_specs, check_vma=False)
```

```python
import functools

import functools

import jax
import jax.numpy as jnp
from jax import lax
from jax.experimental import pallas as pl
from jax.experimental.pallas import tpu as pltpu
from jax.sharding import PartitionSpec as P


BF16 = jnp.bfloat16
F32 = jnp.float32
MIB = 1 << 20


def pair_groups(size, bit):
    step = 1 << bit
    return [[i, i ^ step] for i in range(size) if not i & step]


def axis_of(level, col_bits):
    return ("col", level) if level < col_bits else ("row", level - col_bits)


def both(value, level, col_bits):
    axis, bit = axis_of(level, col_bits)
    groups = pair_groups(lax.axis_size(axis), bit)
    return lax.all_gather(value, axis, axis=0, tiled=False, axis_index_groups=groups)


def among_four(value, level, col_bits):
    axis, bit = axis_of(level, col_bits)
    step, size = 1 << bit, lax.axis_size(axis)
    groups = [[i + step * k for k in range(4)] for i in range(size) if not i & (3 * step)]
    return lax.all_to_all(value, axis, 0, 0, axis_index_groups=groups)


def group_index(level, col_bits):
    axis, bit = axis_of(level, col_bits)
    return lax.rem(lax.div(lax.axis_index(axis), 1 << bit), 4)


def toggle(index, step):
    return step - 2 * step * lax.rem(lax.div(index, step), 2)


def partner_slot(level, col_bits):
    axis, bit = axis_of(level, col_bits)
    return 1 - lax.rem(lax.div(lax.axis_index(axis), 1 << bit), 2)


def times(a, b):
    return jnp.dot(a, b, preferred_element_type=F32)


def times_transposed(a, b):
    return lax.dot_general(a, b, (((0,), (0,)), ((), ())), preferred_element_type=F32)


def pair_sum(pair_ref):
    return pair_ref[0].astype(F32) + pair_ref[1].astype(F32)


def call(kernel, outs, n_in, limit):
    vmem = [pl.BlockSpec(memory_space=pltpu.VMEM)] * n_in
    return pl.pallas_call(
        kernel,
        out_shape=[jax.ShapeDtypeStruct(shape, dtype) for shape, dtype in outs],
        in_specs=vmem,
        out_specs=[pl.BlockSpec(memory_space=pltpu.VMEM)] * len(outs),
        compiler_params=pltpu.CompilerParams(vmem_limit_bytes=limit),
    )


def leaf_kernel(
    low, col_bits, order_hbm, rhs_hbm, inverse_hbm, basis_hbm, up_hbm, down_hbm, rows_hbm, state_hbm, term_ref, share_hbm,
    order_ref, rhs_ref, inverse_ref, basis_ref, up_ref, share_ref, rows_ref, state_ref, sems, share_sems, out_sems,
):
    last = up_hbm.shape[1] - 1
    me = group_index(low, col_bits)
    rows = rhs_ref.shape[0]
    leaves, leaf = inverse_ref.shape[:2]
    moves = [
        pltpu.make_async_copy(src, dst, sems.at[k])
        for k, (src, dst) in enumerate(
            [
                (order_hbm, order_ref),
                (rhs_hbm, rhs_ref),
                (inverse_hbm, inverse_ref),
                (basis_hbm, basis_ref),
                (up_hbm.at[0, 0], up_ref),
                (down_hbm.at[0, last - 1], share_ref.at[0]),
                (up_hbm.at[0, last], share_ref.at[1]),
                (down_hbm.at[0, last], share_ref.at[2]),
            ]
        )
    ]
    for move in moves:
        move.start()
    moves[0].wait()
    across = jnp.broadcast_to(order_ref[...], (128, rows)).T.astype(jnp.int16)
    lane = lax.broadcasted_iota(jnp.int16, (rows, 128), 1)
    pick = jnp.concatenate(
        [jnp.where(across == lane + jnp.int16(128 * b), BF16(1), BF16(0)) for b in range(rows // 128)],
        axis=1,
    )
    moves[1].wait()
    ordered = times(pick, rhs_ref[...]).astype(BF16)
    moves[2].wait()
    moves[3].wait()
    for move in moves[5:]:
        move.wait()
    near, across_pair = me + toggle(me, 1), me + toggle(me, 2)
    slots = [(near, 0), (across_pair, 1), (near + across_pair - me, 1), (me, 1)]
    spread = [
        pltpu.make_async_copy(share_ref.at[first : first + 2], share_hbm.at[slot], share_sems.at[k])
        for k, (slot, first) in enumerate(slots)
    ]
    for move in spread:
        move.start()
    state, keep = None, []
    for j in range(leaves):
        block = times(inverse_ref[j], ordered[j * leaf : (j + 1) * leaf])
        rows_ref[j] = block
        keep.append(pltpu.make_async_copy(rows_ref.at[j], rows_hbm.at[j], out_sems.at[j]))
        keep[-1].start()
        part = times_transposed(basis_ref[j], block.astype(BF16))
        state = part if state is None else state + part
    state_ref[...] = state
    keep.append(pltpu.make_async_copy(state_ref, state_hbm, out_sems.at[leaves]))
    keep[-1].start()
    moves[4].wait()
    term_ref[...] = times(up_ref[...], state.astype(BF16)).astype(BF16)
    for move in spread + keep:
        move.wait()


def up_kernel(level, pair_ref, up_ref, term_ref):
    term_ref[...] = times(up_ref[0, level], pair_sum(pair_ref).astype(BF16)).astype(BF16)


def spread_kernel(level, pair_ref, up_ref, out_ref):
    term = times(up_ref[0, level], pair_sum(pair_ref).astype(BF16)).astype(BF16)
    for k in range(out_ref.shape[0]):
        out_ref[k] = term


def top_kernel(low, col_bits, terms_ref, share_ref, saved_ref, up_ref, down_ref, y_ref, sent_ref):
    me = group_index(low, col_bits)
    flip, across = toggle(me, 1), toggle(me, 2)
    a, b, c, d = me, me + flip, me + across, me + flip + across

    def rounded(x):
        return x.astype(BF16)

    def elim(factor, value):
        return rounded(times(factor, value)).astype(F32)

    def above(factor, coupling, state, value):
        coupled = rounded(times(coupling, value)).astype(F32)
        return rounded(state + 0.5 * (coupled - times_transposed(factor, value)))

    mine, near = up_ref[0, low + 1], share_ref[b, 1]
    state = terms_ref[a].astype(F32) + terms_ref[b].astype(F32)
    far = terms_ref[c].astype(F32) + terms_ref[d].astype(F32)
    state_half, far_half = rounded(state), rounded(far)
    y_mine = rounded(elim(mine, state_half) + elim(share_ref[c, 0], far_half))
    y_near = rounded(elim(near, state_half) + elim(share_ref[d, 0], far_half))
    top_mine = above(mine, share_ref[c, 1], state, y_mine)
    top_near = above(near, share_ref[d, 1], state, y_near)
    coupled = rounded(times(share_ref[b, 0], top_near)).astype(F32)
    top = rounded(pair_sum(saved_ref) + 0.5 * (coupled - times_transposed(up_ref[0, low], top_mine)))
    y_ref[...] = top
    sent_ref[...] = rounded(times(down_ref[0, low - 1], top))


def down_kernel(level, col_bits, pair_ref, saved_ref, above_ref, up_ref, down_ref, y_ref, sent_ref):
    coupled = pair_ref[partner_slot(level, col_bits)].astype(F32)
    top = pair_sum(saved_ref) + 0.5 * (coupled - times_transposed(up_ref[0, level], above_ref[...]))
    y_ref[...] = top.astype(BF16)
    sent_ref[...] = times(down_ref[0, level - 1], top.astype(BF16)).astype(BF16)


def last_kernel(
    col_bits, order_ref, pair_ref, state_ref, above_ref, up_ref, inverse_ref, basis_ref, rows_ref, out_ref
):
    rows = out_ref.shape[0]
    leaves = inverse_ref.shape[0]
    coupled = pair_ref[partner_slot(0, col_bits)].astype(F32)
    top = state_ref[...] + 0.5 * (coupled - times_transposed(up_ref[0, 0], above_ref[...]))
    top_half = top.astype(BF16)
    solved = []
    for j in range(leaves):
        back = times(basis_ref[j], top_half).astype(BF16)
        solved.append((rows_ref[j] - times(inverse_ref[j], back)).astype(BF16))
    place = lax.broadcasted_iota(jnp.int16, (rows, rows), 0) == order_ref[...].astype(jnp.int16)
    pick = jnp.where(place, BF16(1), BF16(0))
    out_ref[...] = times(pick, jnp.concatenate(solved, axis=0)).astype(BF16)


def on_device(
    rhs, order, leaf_inverse, leaf_column_generator, factor_up, downward_coupling_factors
):
    leaves, leaf = leaf_inverse.shape[:2]
    rank = leaf_column_generator.shape[2]
    genes = rhs.shape[1]
    levels = factor_up.shape[1]
    last = levels - 1
    low = last - 1
    col_bits = lax.axis_size("col").bit_length() - 1
    up, down = factor_up, downward_coupling_factors
    small = (rank, genes)
    steps = [(small, BF16), (small, BF16)]

    rows, state, term, share = pl.pallas_call(
        functools.partial(leaf_kernel, low, col_bits),
        out_shape=[
            jax.ShapeDtypeStruct((leaves, leaf, genes), F32),
            jax.ShapeDtypeStruct(small, F32),
            jax.ShapeDtypeStruct(small, BF16),
            jax.ShapeDtypeStruct((4, 2) + factor_up.shape[2:], BF16),
        ],
        in_specs=[pl.BlockSpec(memory_space=pltpu.HBM)] * 6,
        out_specs=[pl.BlockSpec(memory_space=pltpu.VMEM if k == 2 else pltpu.HBM) for k in range(4)],
        scratch_shapes=[
            pltpu.VMEM(order.shape, order.dtype),
            pltpu.VMEM(rhs.shape, BF16),
            pltpu.VMEM(leaf_inverse.shape, BF16),
            pltpu.VMEM(leaf_column_generator.shape, BF16),
            pltpu.VMEM(factor_up.shape[2:], BF16),
            pltpu.VMEM((3,) + factor_up.shape[2:], BF16),
            pltpu.VMEM((leaves, leaf, genes), F32),
            pltpu.VMEM(small, F32),
            pltpu.SemaphoreType.DMA((8,)),
            pltpu.SemaphoreType.DMA((4,)),
            pltpu.SemaphoreType.DMA((leaves + 1,)),
        ],
        compiler_params=pltpu.CompilerParams(vmem_limit_bytes=56 * MIB),
    )(order, rhs, leaf_inverse, leaf_column_generator, up, down)
    pairs = [both(term, 0, col_bits)]
    shared = among_four(share, low, col_bits)
    for level in range(1, low):
        (term,) = call(functools.partial(up_kernel, level), [(small, BF16)], 2, 4 * MIB)(pairs[-1], up)
        pairs.append(both(term, level, col_bits))
        if level == low - 1:
            pairs[-1], shared = lax.optimization_barrier((pairs[-1], shared))
    (terms,) = call(functools.partial(spread_kernel, low), [((4,) + small, BF16)], 2, 4 * MIB)(pairs[-1], up)
    y, sent = call(functools.partial(top_kernel, low, col_bits), steps, 5, 8 * MIB)(
        among_four(terms, low, col_bits), shared, pairs[-1], up, down
    )
    for level in range(low - 1, 0, -1):
        y, sent = call(functools.partial(down_kernel, level, col_bits), steps, 5, 6 * MIB)(
            both(sent, level, col_bits), pairs[level - 1], y, up, down
        )
    (solved,) = call(functools.partial(last_kernel, col_bits), [(rhs.shape, BF16)], 8, 24 * MIB)(
        order, both(sent, 0, col_bits), state, y, up, leaf_inverse, leaf_column_generator, rows
    )
    return solved


def solution(mesh):
    in_specs = (
        P(("row", "col"), None),
        P(("row", "col"), None),
        P(("row", "col"), None, None),
        P(("row", "col"), None, None),
        P(("row", "col"), None, None, None),
        P(("row", "col"), None, None, None),
    )
    out_specs = P(("row", "col"), None)

    return jax.shard_map(on_device, mesh=mesh, in_specs=in_specs, out_specs=out_specs, check_vma=False)
```

```python
import functools

import functools

import jax
import jax.numpy as jnp
from jax import lax
from jax.experimental import pallas as pl
from jax.experimental.pallas import tpu as pltpu
from jax.sharding import PartitionSpec as P


BF16 = jnp.bfloat16
F32 = jnp.float32
MIB = 1 << 20


def pair_groups(size, bit):
    step = 1 << bit
    return [[i, i ^ step] for i in range(size) if not i & step]


def axis_of(level, col_bits):
    return ("col", level) if level < col_bits else ("row", level - col_bits)


def both(value, level, col_bits):
    axis, bit = axis_of(level, col_bits)
    groups = pair_groups(lax.axis_size(axis), bit)
    return lax.all_gather(value, axis, axis=0, tiled=False, axis_index_groups=groups)


def across_both(value, level, col_bits):
    axis, bit = axis_of(level, col_bits)
    step, size = 1 << bit, lax.axis_size(axis)
    groups = [[i, i ^ (3 * step)] for i in range(size) if not i & (2 * step)]
    return lax.all_gather(value, axis, axis=0, tiled=False, axis_index_groups=groups)


def among_four(value, level, col_bits):
    axis, bit = axis_of(level, col_bits)
    step, size = 1 << bit, lax.axis_size(axis)
    groups = [[i + step * k for k in range(4)] for i in range(size) if not i & (3 * step)]
    return lax.all_to_all(value, axis, 0, 0, axis_index_groups=groups)


def group_index(level, col_bits):
    axis, bit = axis_of(level, col_bits)
    return lax.rem(lax.div(lax.axis_index(axis), 1 << bit), 4)


def toggle(index, step):
    return step - 2 * step * lax.rem(lax.div(index, step), 2)


def partner_slot(level, col_bits):
    axis, bit = axis_of(level, col_bits)
    return 1 - lax.rem(lax.div(lax.axis_index(axis), 1 << bit), 2)


def times(a, b):
    return jnp.dot(a, b, preferred_element_type=F32)


def times_transposed(a, b):
    return lax.dot_general(a, b, (((0,), (0,)), ((), ())), preferred_element_type=F32)


def pair_sum(pair_ref):
    return pair_ref[0].astype(F32) + pair_ref[1].astype(F32)


def call(kernel, outs, n_in, limit):
    vmem = [pl.BlockSpec(memory_space=pltpu.VMEM)] * n_in
    return pl.pallas_call(
        kernel,
        out_shape=[jax.ShapeDtypeStruct(shape, dtype) for shape, dtype in outs],
        in_specs=vmem,
        out_specs=[pl.BlockSpec(memory_space=pltpu.VMEM)] * len(outs),
        compiler_params=pltpu.CompilerParams(vmem_limit_bytes=limit),
    )


def leaf_kernel(
    low, col_bits, order_hbm, rhs_hbm, inverse_hbm, basis_hbm, up_hbm, down_hbm, rows_hbm, state_hbm, term_ref, share_hbm,
    order_ref, rhs_ref, inverse_ref, basis_ref, up_ref, share_ref, rows_ref, state_ref, sems, share_sems, out_sems,
):
    last = up_hbm.shape[1] - 1
    me = group_index(low, col_bits)
    rows = rhs_ref.shape[0]
    leaves, leaf = inverse_ref.shape[:2]
    moves = [
        pltpu.make_async_copy(src, dst, sems.at[k])
        for k, (src, dst) in enumerate(
            [
                (order_hbm, order_ref),
                (rhs_hbm, rhs_ref),
                (inverse_hbm, inverse_ref),
                (basis_hbm, basis_ref),
                (up_hbm.at[0, 0], up_ref),
                (down_hbm.at[0, last - 1], share_ref.at[0]),
                (up_hbm.at[0, last], share_ref.at[1]),
                (down_hbm.at[0, last], share_ref.at[2]),
            ]
        )
    ]
    for move in moves:
        move.start()
    moves[0].wait()
    across = jnp.broadcast_to(order_ref[...], (128, rows)).T.astype(jnp.int16)
    lane = lax.broadcasted_iota(jnp.int16, (rows, 128), 1)
    pick = jnp.concatenate(
        [jnp.where(across == lane + jnp.int16(128 * b), BF16(1), BF16(0)) for b in range(rows // 128)],
        axis=1,
    )
    moves[1].wait()
    ordered = times(pick, rhs_ref[...]).astype(BF16)
    moves[2].wait()
    moves[3].wait()
    for move in moves[5:]:
        move.wait()
    near, across_pair = me + toggle(me, 1), me + toggle(me, 2)
    slots = [(near, 0), (across_pair, 1), (near + across_pair - me, 1), (me, 1)]
    spread = [
        pltpu.make_async_copy(share_ref.at[first : first + 2], share_hbm.at[slot], share_sems.at[k])
        for k, (slot, first) in enumerate(slots)
    ]
    for move in spread:
        move.start()
    state, keep = None, []
    for j in range(leaves):
        block = times(inverse_ref[j], ordered[j * leaf : (j + 1) * leaf])
        rows_ref[j] = block
        keep.append(pltpu.make_async_copy(rows_ref.at[j], rows_hbm.at[j], out_sems.at[j]))
        keep[-1].start()
        part = times_transposed(basis_ref[j], block.astype(BF16))
        state = part if state is None else state + part
    state_ref[...] = state
    keep.append(pltpu.make_async_copy(state_ref, state_hbm, out_sems.at[leaves]))
    keep[-1].start()
    moves[4].wait()
    term_ref[...] = times(up_ref[...], state.astype(BF16)).astype(BF16)
    for move in spread + keep:
        move.wait()


def up_kernel(level, pair_ref, up_ref, term_ref):
    term_ref[...] = times(up_ref[0, level], pair_sum(pair_ref).astype(BF16)).astype(BF16)


def state_kernel(pair_ref, half_ref):
    half_ref[...] = pair_sum(pair_ref).astype(BF16)


def top_kernel(low, col_bits, terms_ref, half_ref, share_ref, saved_ref, up_ref, down_ref, y_ref, sent_ref):
    me = group_index(low, col_bits)
    flip, across = toggle(me, 1), toggle(me, 2)
    b, c, d = me + flip, me + across, me + flip + across

    def rounded(x):
        return x.astype(BF16)

    def elim(factor, value):
        return rounded(times(factor, value)).astype(F32)

    def above(factor, coupling, state, value):
        coupled = rounded(times(coupling, value)).astype(F32)
        return rounded(state + 0.5 * (coupled - times_transposed(factor, value)))

    mine, near = up_ref[0, low + 1], share_ref[b, 1]
    state = pair_sum(terms_ref)
    other = 1 - lax.div(me, 2)
    state_half, far_half = half_ref[1 - other], half_ref[other]
    y_mine = rounded(elim(mine, state_half) + elim(share_ref[c, 0], far_half))
    y_near = rounded(elim(near, state_half) + elim(share_ref[d, 0], far_half))
    top_mine = above(mine, share_ref[c, 1], state, y_mine)
    top_near = above(near, share_ref[d, 1], state, y_near)
    coupled = rounded(times(share_ref[b, 0], top_near)).astype(F32)
    top = rounded(pair_sum(saved_ref) + 0.5 * (coupled - times_transposed(up_ref[0, low], top_mine)))
    y_ref[...] = top
    sent_ref[...] = rounded(times(down_ref[0, low - 1], top))


def down_kernel(level, col_bits, pair_ref, saved_ref, above_ref, up_ref, down_ref, y_ref, sent_ref):
    coupled = pair_ref[partner_slot(level, col_bits)].astype(F32)
    top = pair_sum(saved_ref) + 0.5 * (coupled - times_transposed(up_ref[0, level], above_ref[...]))
    y_ref[...] = top.astype(BF16)
    sent_ref[...] = times(down_ref[0, level - 1], top.astype(BF16)).astype(BF16)


def last_kernel(
    col_bits, order_ref, pair_ref, state_ref, above_ref, up_ref, inverse_ref, basis_ref, rows_ref, out_ref
):
    rows = out_ref.shape[0]
    leaves = inverse_ref.shape[0]
    coupled = pair_ref[partner_slot(0, col_bits)].astype(F32)
    top = state_ref[...] + 0.5 * (coupled - times_transposed(up_ref[0, 0], above_ref[...]))
    top_half = top.astype(BF16)
    solved = []
    for j in range(leaves):
        back = times(basis_ref[j], top_half).astype(BF16)
        solved.append((rows_ref[j] - times(inverse_ref[j], back)).astype(BF16))
    place = lax.broadcasted_iota(jnp.int16, (rows, rows), 0) == order_ref[...].astype(jnp.int16)
    pick = jnp.where(place, BF16(1), BF16(0))
    out_ref[...] = times(pick, jnp.concatenate(solved, axis=0)).astype(BF16)


def on_device(
    rhs, order, leaf_inverse, leaf_column_generator, factor_up, downward_coupling_factors
):
    leaves, leaf = leaf_inverse.shape[:2]
    rank = leaf_column_generator.shape[2]
    genes = rhs.shape[1]
    levels = factor_up.shape[1]
    last = levels - 1
    low = last - 1
    col_bits = lax.axis_size("col").bit_length() - 1
    up, down = factor_up, downward_coupling_factors
    small = (rank, genes)
    steps = [(small, BF16), (small, BF16)]

    rows, state, term, share = pl.pallas_call(
        functools.partial(leaf_kernel, low, col_bits),
        out_shape=[
            jax.ShapeDtypeStruct((leaves, leaf, genes), F32),
            jax.ShapeDtypeStruct(small, F32),
            jax.ShapeDtypeStruct(small, BF16),
            jax.ShapeDtypeStruct((4, 2) + factor_up.shape[2:], BF16),
        ],
        in_specs=[pl.BlockSpec(memory_space=pltpu.HBM)] * 6,
        out_specs=[pl.BlockSpec(memory_space=pltpu.VMEM if k == 2 else pltpu.HBM) for k in range(4)],
        scratch_shapes=[
            pltpu.VMEM(order.shape, order.dtype),
            pltpu.VMEM(rhs.shape, BF16),
            pltpu.VMEM(leaf_inverse.shape, BF16),
            pltpu.VMEM(leaf_column_generator.shape, BF16),
            pltpu.VMEM(factor_up.shape[2:], BF16),
            pltpu.VMEM((3,) + factor_up.shape[2:], BF16),
            pltpu.VMEM((leaves, leaf, genes), F32),
            pltpu.VMEM(small, F32),
            pltpu.SemaphoreType.DMA((8,)),
            pltpu.SemaphoreType.DMA((4,)),
            pltpu.SemaphoreType.DMA((leaves + 1,)),
        ],
        compiler_params=pltpu.CompilerParams(vmem_limit_bytes=56 * MIB),
    )(order, rhs, leaf_inverse, leaf_column_generator, up, down)
    pairs = [both(term, 0, col_bits)]
    shared = among_four(share, low, col_bits)
    for level in range(1, low):
        (term,) = call(functools.partial(up_kernel, level), [(small, BF16)], 2, 4 * MIB)(pairs[-1], up)
        pairs.append(both(term, level, col_bits))
    (term,) = call(functools.partial(up_kernel, low), [(small, BF16)], 2, 4 * MIB)(pairs[-1], up)
    term, shared = lax.optimization_barrier((term, shared))
    terms = both(term, low, col_bits)
    (half,) = call(state_kernel, [(small, BF16)], 1, 4 * MIB)(terms)
    y, sent = call(functools.partial(top_kernel, low, col_bits), steps, 6, 8 * MIB)(
        terms, across_both(half, low, col_bits), shared, pairs[-1], up, down
    )
    for level in range(low - 1, 0, -1):
        y, sent = call(functools.partial(down_kernel, level, col_bits), steps, 5, 6 * MIB)(
            both(sent, level, col_bits), pairs[level - 1], y, up, down
        )
    (solved,) = call(functools.partial(last_kernel, col_bits), [(rhs.shape, BF16)], 8, 24 * MIB)(
        order, both(sent, 0, col_bits), state, y, up, leaf_inverse, leaf_column_generator, rows
    )
    return solved


def solution(mesh):
    in_specs = (
        P(("row", "col"), None),
        P(("row", "col"), None),
        P(("row", "col"), None, None),
        P(("row", "col"), None, None),
        P(("row", "col"), None, None, None),
        P(("row", "col"), None, None, None),
    )
    out_specs = P(("row", "col"), None)

    return jax.shard_map(on_device, mesh=mesh, in_specs=in_specs, out_specs=out_specs, check_vma=False)
```

```python
import functools

import functools

import jax
import jax.numpy as jnp
from jax import lax
from jax.experimental import pallas as pl
from jax.experimental.pallas import tpu as pltpu
from jax.sharding import PartitionSpec as P


BF16 = jnp.bfloat16
F32 = jnp.float32
MIB = 1 << 20


def pair_groups(size, bit):
    step = 1 << bit
    return [[i, i ^ step] for i in range(size) if not i & step]


def axis_of(level, col_bits):
    return ("col", level) if level < col_bits else ("row", level - col_bits)


def both(value, level, col_bits):
    axis, bit = axis_of(level, col_bits)
    groups = pair_groups(lax.axis_size(axis), bit)
    return lax.all_gather(value, axis, axis=0, tiled=False, axis_index_groups=groups)


def across_both(value, level, col_bits):
    axis, bit = axis_of(level, col_bits)
    step, size = 1 << bit, lax.axis_size(axis)
    groups = [[i, i ^ (3 * step)] for i in range(size) if not i & (2 * step)]
    return lax.all_gather(value, axis, axis=0, tiled=False, axis_index_groups=groups)


def among_four(value, level, col_bits):
    axis, bit = axis_of(level, col_bits)
    step, size = 1 << bit, lax.axis_size(axis)
    groups = [[i + step * k for k in range(4)] for i in range(size) if not i & (3 * step)]
    return lax.all_to_all(value, axis, 0, 0, axis_index_groups=groups)


def group_index(level, col_bits):
    axis, bit = axis_of(level, col_bits)
    return lax.rem(lax.div(lax.axis_index(axis), 1 << bit), 4)


def toggle(index, step):
    return step - 2 * step * lax.rem(lax.div(index, step), 2)


def partner_slot(level, col_bits):
    axis, bit = axis_of(level, col_bits)
    return 1 - lax.rem(lax.div(lax.axis_index(axis), 1 << bit), 2)


def times(a, b):
    return jnp.dot(a, b, preferred_element_type=F32)


def times_transposed(a, b):
    return lax.dot_general(a, b, (((0,), (0,)), ((), ())), preferred_element_type=F32)


def pair_sum(pair_ref):
    return pair_ref[0].astype(F32) + pair_ref[1].astype(F32)


def call(kernel, outs, n_in, limit):
    vmem = [pl.BlockSpec(memory_space=pltpu.VMEM)] * n_in
    return pl.pallas_call(
        kernel,
        out_shape=[jax.ShapeDtypeStruct(shape, dtype) for shape, dtype in outs],
        in_specs=vmem,
        out_specs=[pl.BlockSpec(memory_space=pltpu.VMEM)] * len(outs),
        compiler_params=pltpu.CompilerParams(vmem_limit_bytes=limit),
    )


def leaf_kernel(
    low, col_bits, order_hbm, rhs_hbm, inverse_hbm, basis_hbm, up_hbm, down_hbm, rows_hbm, state_hbm, term_ref, share_hbm,
    order_ref, rhs_ref, inverse_ref, basis_ref, up_ref, share_ref, rows_ref, state_ref, sems, share_sems, out_sems,
):
    last = up_hbm.shape[1] - 1
    me = group_index(low, col_bits)
    rows = rhs_ref.shape[0]
    leaves, leaf = inverse_ref.shape[:2]
    moves = [
        pltpu.make_async_copy(src, dst, sems.at[k])
        for k, (src, dst) in enumerate(
            [
                (order_hbm, order_ref),
                (rhs_hbm, rhs_ref),
                (inverse_hbm, inverse_ref),
                (basis_hbm, basis_ref),
                (up_hbm.at[0, 0], up_ref),
                (down_hbm.at[0, last - 1], share_ref.at[0]),
                (up_hbm.at[0, last], share_ref.at[1]),
                (down_hbm.at[0, last], share_ref.at[2]),
            ]
        )
    ]
    for move in moves:
        move.start()
    moves[0].wait()
    across = jnp.broadcast_to(order_ref[...], (128, rows)).T.astype(jnp.int16)
    lane = lax.broadcasted_iota(jnp.int16, (rows, 128), 1)
    pick = jnp.concatenate(
        [jnp.where(across == lane + jnp.int16(128 * b), BF16(1), BF16(0)) for b in range(rows // 128)],
        axis=1,
    )
    moves[1].wait()
    ordered = times(pick, rhs_ref[...]).astype(BF16)
    moves[2].wait()
    moves[3].wait()
    for move in moves[5:]:
        move.wait()
    near, across_pair = me + toggle(me, 1), me + toggle(me, 2)
    slots = [(near, 0), (across_pair, 1), (near + across_pair - me, 1), (me, 1)]
    spread = [
        pltpu.make_async_copy(share_ref.at[first : first + 2], share_hbm.at[slot], share_sems.at[k])
        for k, (slot, first) in enumerate(slots)
    ]
    for move in spread:
        move.start()
    state, keep = None, []
    for j in range(leaves):
        block = times(inverse_ref[j], ordered[j * leaf : (j + 1) * leaf])
        rows_ref[j] = block
        keep.append(pltpu.make_async_copy(rows_ref.at[j], rows_hbm.at[j], out_sems.at[j]))
        keep[-1].start()
        part = times_transposed(basis_ref[j], block.astype(BF16))
        state = part if state is None else state + part
    state_ref[...] = state
    keep.append(pltpu.make_async_copy(state_ref, state_hbm, out_sems.at[leaves]))
    keep[-1].start()
    moves[4].wait()
    term_ref[...] = times(up_ref[...], state.astype(BF16)).astype(BF16)
    for move in spread + keep:
        move.wait()


def up_kernel(level, pair_ref, up_ref, term_ref):
    term_ref[...] = times(up_ref[0, level], pair_sum(pair_ref).astype(BF16)).astype(BF16)


def state_kernel(pair_ref, half_ref):
    half_ref[...] = pair_sum(pair_ref).astype(BF16)


def top_kernel(low, col_bits, terms_ref, half_ref, share_ref, saved_ref, up_ref, down_ref, y_ref, sent_ref):
    me = group_index(low, col_bits)
    flip, across = toggle(me, 1), toggle(me, 2)
    b, c, d = me + flip, me + across, me + flip + across

    def rounded(x):
        return x.astype(BF16)

    def elim(factor, value):
        return rounded(times(factor, value)).astype(F32)

    def above(factor, coupling, state, value):
        coupled = rounded(times(coupling, value)).astype(F32)
        return rounded(state + 0.5 * (coupled - times_transposed(factor, value)))

    mine, near = up_ref[0, low + 1], share_ref[b, 1]
    state = pair_sum(terms_ref)
    other = 1 - lax.div(me, 2)
    state_half, far_half = half_ref[1 - other], half_ref[other]
    y_mine = rounded(elim(mine, state_half) + elim(share_ref[c, 0], far_half))
    y_near = rounded(elim(near, state_half) + elim(share_ref[d, 0], far_half))
    top_mine = above(mine, share_ref[c, 1], state, y_mine)
    top_near = above(near, share_ref[d, 1], state, y_near)
    coupled = rounded(times(share_ref[b, 0], top_near)).astype(F32)
    top = rounded(pair_sum(saved_ref) + 0.5 * (coupled - times_transposed(up_ref[0, low], top_mine)))
    y_ref[...] = top
    sent_ref[...] = rounded(times(down_ref[0, low - 1], top))


def down_kernel(level, col_bits, pair_ref, saved_ref, above_ref, up_ref, down_ref, y_ref, sent_ref):
    coupled = pair_ref[partner_slot(level, col_bits)].astype(F32)
    top = pair_sum(saved_ref) + 0.5 * (coupled - times_transposed(up_ref[0, level], above_ref[...]))
    y_ref[...] = top.astype(BF16)
    sent_ref[...] = times(down_ref[0, level - 1], top.astype(BF16)).astype(BF16)


def last_kernel(
    col_bits, order_ref, pair_ref, state_ref, above_ref, up_ref, inverse_ref, basis_ref, rows_ref, out_hbm, out_ref, sems
):
    rows = out_ref.shape[0]
    leaves = inverse_ref.shape[0]
    coupled = pair_ref[partner_slot(0, col_bits)].astype(F32)
    top = state_ref[...] + 0.5 * (coupled - times_transposed(up_ref[0, 0], above_ref[...]))
    top_half = top.astype(BF16)
    solved = []
    for j in range(leaves):
        back = times(basis_ref[j], top_half).astype(BF16)
        solved.append((rows_ref[j] - times(inverse_ref[j], back)).astype(BF16))
    place = lax.broadcasted_iota(jnp.int16, (rows, rows), 0) == order_ref[...].astype(jnp.int16)
    pick = jnp.where(place, BF16(1), BF16(0))
    solved = jnp.concatenate(solved, axis=0)
    half = rows // 2
    moves = []
    for k in range(2):
        part = pl.ds(k * half, half)
        out_ref[part] = times(pick[k * half : (k + 1) * half], solved).astype(BF16)
        moves.append(pltpu.make_async_copy(out_ref.at[part], out_hbm.at[part], sems.at[k]))
        moves[-1].start()
    for move in moves:
        move.wait()


def on_device(
    rhs, order, leaf_inverse, leaf_column_generator, factor_up, downward_coupling_factors
):
    leaves, leaf = leaf_inverse.shape[:2]
    rank = leaf_column_generator.shape[2]
    genes = rhs.shape[1]
    levels = factor_up.shape[1]
    last = levels - 1
    low = last - 1
    col_bits = lax.axis_size("col").bit_length() - 1
    up, down = factor_up, downward_coupling_factors
    small = (rank, genes)
    steps = [(small, BF16), (small, BF16)]

    rows, state, term, share = pl.pallas_call(
        functools.partial(leaf_kernel, low, col_bits),
        out_shape=[
            jax.ShapeDtypeStruct((leaves, leaf, genes), F32),
            jax.ShapeDtypeStruct(small, F32),
            jax.ShapeDtypeStruct(small, BF16),
            jax.ShapeDtypeStruct((4, 2) + factor_up.shape[2:], BF16),
        ],
        in_specs=[pl.BlockSpec(memory_space=pltpu.HBM)] * 6,
        out_specs=[pl.BlockSpec(memory_space=pltpu.VMEM if k == 2 else pltpu.HBM) for k in range(4)],
        scratch_shapes=[
            pltpu.VMEM(order.shape, order.dtype),
            pltpu.VMEM(rhs.shape, BF16),
            pltpu.VMEM(leaf_inverse.shape, BF16),
            pltpu.VMEM(leaf_column_generator.shape, BF16),
            pltpu.VMEM(factor_up.shape[2:], BF16),
            pltpu.VMEM((3,) + factor_up.shape[2:], BF16),
            pltpu.VMEM((leaves, leaf, genes), F32),
            pltpu.VMEM(small, F32),
            pltpu.SemaphoreType.DMA((8,)),
            pltpu.SemaphoreType.DMA((4,)),
            pltpu.SemaphoreType.DMA((leaves + 1,)),
        ],
        compiler_params=pltpu.CompilerParams(vmem_limit_bytes=56 * MIB),
    )(order, rhs, leaf_inverse, leaf_column_generator, up, down)
    term, up = lax.optimization_barrier((term, up))
    pairs = [both(term, 0, col_bits)]
    shared = among_four(share, low, col_bits)
    for level in range(1, low):
        (term,) = call(functools.partial(up_kernel, level), [(small, BF16)], 2, 4 * MIB)(pairs[-1], up)
        pairs.append(both(term, level, col_bits))
    (term,) = call(functools.partial(up_kernel, low), [(small, BF16)], 2, 4 * MIB)(pairs[-1], up)
    term, shared = lax.optimization_barrier((term, shared))
    terms = both(term, low, col_bits)
    (half,) = call(state_kernel, [(small, BF16)], 1, 4 * MIB)(terms)
    y, sent = call(functools.partial(top_kernel, low, col_bits), steps, 6, 8 * MIB)(
        terms, across_both(half, low, col_bits), shared, pairs[-1], up, down
    )
    for level in range(low - 1, 0, -1):
        y, sent = call(functools.partial(down_kernel, level, col_bits), steps, 5, 6 * MIB)(
            both(sent, level, col_bits), pairs[level - 1], y, up, down
        )
    (solved,) = pl.pallas_call(
        functools.partial(last_kernel, col_bits),
        out_shape=[jax.ShapeDtypeStruct(rhs.shape, BF16)],
        in_specs=[pl.BlockSpec(memory_space=pltpu.VMEM)] * 8,
        out_specs=[pl.BlockSpec(memory_space=pltpu.HBM)],
        scratch_shapes=[pltpu.VMEM(rhs.shape, BF16), pltpu.SemaphoreType.DMA((2,))],
        compiler_params=pltpu.CompilerParams(vmem_limit_bytes=24 * MIB),
    )(order, both(sent, 0, col_bits), state, y, up, leaf_inverse, leaf_column_generator, rows)
    return solved


def solution(mesh):
    in_specs = (
        P(("row", "col"), None),
        P(("row", "col"), None),
        P(("row", "col"), None, None),
        P(("row", "col"), None, None),
        P(("row", "col"), None, None, None),
        P(("row", "col"), None, None, None),
    )
    out_specs = P(("row", "col"), None)

    return jax.shard_map(on_device, mesh=mesh, in_specs=in_specs, out_specs=out_specs, check_vma=False)
```

```python
import functools

import functools

import jax
import jax.numpy as jnp
from jax import lax
from jax.experimental import pallas as pl
from jax.experimental.pallas import tpu as pltpu
from jax.sharding import PartitionSpec as P


BF16 = jnp.bfloat16
F32 = jnp.float32
MIB = 1 << 20


def pair_groups(size, bit):
    step = 1 << bit
    return [[i, i ^ step] for i in range(size) if not i & step]


def axis_of(level, col_bits):
    return ("col", level) if level < col_bits else ("row", level - col_bits)


def both(value, level, col_bits):
    axis, bit = axis_of(level, col_bits)
    groups = pair_groups(lax.axis_size(axis), bit)
    return lax.all_gather(value, axis, axis=0, tiled=False, axis_index_groups=groups)


def across_both(value, level, col_bits):
    axis, bit = axis_of(level, col_bits)
    step, size = 1 << bit, lax.axis_size(axis)
    groups = [[i, i ^ (3 * step)] for i in range(size) if not i & (2 * step)]
    return lax.all_gather(value, axis, axis=0, tiled=False, axis_index_groups=groups)


def among_four(value, level, col_bits):
    axis, bit = axis_of(level, col_bits)
    step, size = 1 << bit, lax.axis_size(axis)
    groups = [[i + step * k for k in range(4)] for i in range(size) if not i & (3 * step)]
    return lax.all_to_all(value, axis, 0, 0, axis_index_groups=groups)


def group_index(level, col_bits):
    axis, bit = axis_of(level, col_bits)
    return lax.rem(lax.div(lax.axis_index(axis), 1 << bit), 4)


def toggle(index, step):
    return step - 2 * step * lax.rem(lax.div(index, step), 2)


def partner_slot(level, col_bits):
    axis, bit = axis_of(level, col_bits)
    return 1 - lax.rem(lax.div(lax.axis_index(axis), 1 << bit), 2)


def times(a, b):
    return jnp.dot(a, b, preferred_element_type=F32)


def times_transposed(a, b):
    return lax.dot_general(a, b, (((0,), (0,)), ((), ())), preferred_element_type=F32)


def pair_sum(pair_ref):
    return pair_ref[0].astype(F32) + pair_ref[1].astype(F32)


def call(kernel, outs, n_in, limit):
    vmem = [pl.BlockSpec(memory_space=pltpu.VMEM)] * n_in
    return pl.pallas_call(
        kernel,
        out_shape=[jax.ShapeDtypeStruct(shape, dtype) for shape, dtype in outs],
        in_specs=vmem,
        out_specs=[pl.BlockSpec(memory_space=pltpu.VMEM)] * len(outs),
        compiler_params=pltpu.CompilerParams(vmem_limit_bytes=limit),
    )


def leaf_kernel(
    low, col_bits, order_hbm, rhs_hbm, inverse_hbm, basis_hbm, up_hbm, down_hbm, rows_hbm, state_hbm, term_ref, share_hbm,
    order_ref, rhs_ref, inverse_ref, basis_ref, up_ref, share_ref, rows_ref, state_ref, sems, share_sems, out_sems,
):
    last = up_hbm.shape[1] - 1
    me = group_index(low, col_bits)
    rows = rhs_ref.shape[0]
    leaves, leaf = inverse_ref.shape[:2]
    moves = [
        pltpu.make_async_copy(src, dst, sems.at[k])
        for k, (src, dst) in enumerate(
            [
                (order_hbm, order_ref),
                (rhs_hbm, rhs_ref),
                (inverse_hbm, inverse_ref),
                (basis_hbm, basis_ref),
                (up_hbm.at[0, 0], up_ref),
                (down_hbm.at[0, last - 1], share_ref.at[0]),
                (up_hbm.at[0, last], share_ref.at[1]),
                (down_hbm.at[0, last], share_ref.at[2]),
            ]
        )
    ]
    for move in moves:
        move.start()
    moves[0].wait()
    across = jnp.broadcast_to(order_ref[...], (128, rows)).T.astype(jnp.int16)
    lane = lax.broadcasted_iota(jnp.int16, (rows, 128), 1)
    pick = jnp.concatenate(
        [jnp.where(across == lane + jnp.int16(128 * b), BF16(1), BF16(0)) for b in range(rows // 128)],
        axis=1,
    )
    moves[1].wait()
    ordered = times(pick, rhs_ref[...]).astype(BF16)
    moves[2].wait()
    moves[3].wait()
    for move in moves[5:]:
        move.wait()
    near, across_pair = me + toggle(me, 1), me + toggle(me, 2)
    slots = [(near, 0), (across_pair, 1), (near + across_pair - me, 1), (me, 1)]
    spread = [
        pltpu.make_async_copy(share_ref.at[first : first + 2], share_hbm.at[slot], share_sems.at[k])
        for k, (slot, first) in enumerate(slots)
    ]
    for move in spread:
        move.start()
    state, keep = None, []
    for j in range(leaves):
        block = times(inverse_ref[j], ordered[j * leaf : (j + 1) * leaf])
        rows_ref[j] = block
        keep.append(pltpu.make_async_copy(rows_ref.at[j], rows_hbm.at[j], out_sems.at[j]))
        keep[-1].start()
        part = times_transposed(basis_ref[j], block.astype(BF16))
        state = part if state is None else state + part
    state_ref[...] = state
    keep.append(pltpu.make_async_copy(state_ref, state_hbm, out_sems.at[leaves]))
    keep[-1].start()
    moves[4].wait()
    term_ref[...] = times(up_ref[...], state.astype(BF16)).astype(BF16)
    for move in spread + keep:
        move.wait()


def up_kernel(level, pair_ref, up_ref, term_ref):
    term_ref[...] = times(up_ref[0, level], pair_sum(pair_ref).astype(BF16)).astype(BF16)


def state_kernel(pair_ref, half_ref):
    half_ref[...] = pair_sum(pair_ref).astype(BF16)


def top_kernel(low, col_bits, terms_ref, half_ref, share_ref, saved_ref, up_ref, down_ref, y_ref, sent_ref):
    me = group_index(low, col_bits)
    flip, across = toggle(me, 1), toggle(me, 2)
    b, c, d = me + flip, me + across, me + flip + across

    def rounded(x):
        return x.astype(BF16)

    def elim(factor, value):
        return rounded(times(factor, value)).astype(F32)

    def above(factor, coupling, state, value):
        coupled = rounded(times(coupling, value)).astype(F32)
        return rounded(state + 0.5 * (coupled - times_transposed(factor, value)))

    mine, near = up_ref[0, low + 1], share_ref[b, 1]
    state = pair_sum(terms_ref)
    other = 1 - lax.div(me, 2)
    state_half, far_half = half_ref[1 - other], half_ref[other]
    y_mine = rounded(elim(mine, state_half) + elim(share_ref[c, 0], far_half))
    y_near = rounded(elim(near, state_half) + elim(share_ref[d, 0], far_half))
    top_mine = above(mine, share_ref[c, 1], state, y_mine)
    top_near = above(near, share_ref[d, 1], state, y_near)
    coupled = rounded(times(share_ref[b, 0], top_near)).astype(F32)
    top = rounded(pair_sum(saved_ref) + 0.5 * (coupled - times_transposed(up_ref[0, low], top_mine)))
    y_ref[...] = top
    sent_ref[...] = rounded(times(down_ref[0, low - 1], top))


def down_kernel(level, col_bits, pair_ref, saved_ref, above_ref, up_ref, down_ref, y_ref, sent_ref):
    coupled = pair_ref[partner_slot(level, col_bits)].astype(F32)
    top = pair_sum(saved_ref) + 0.5 * (coupled - times_transposed(up_ref[0, level], above_ref[...]))
    y_ref[...] = top.astype(BF16)
    sent_ref[...] = times(down_ref[0, level - 1], top.astype(BF16)).astype(BF16)


def last_kernel(
    col_bits, order_ref, pair_ref, state_ref, above_ref, up_ref, inverse_ref, basis_ref, rows_ref, out_hbm, out_ref, sems
):
    rows = out_ref.shape[0]
    leaves = inverse_ref.shape[0]
    coupled = pair_ref[partner_slot(0, col_bits)].astype(F32)
    top = state_ref[...] + 0.5 * (coupled - times_transposed(up_ref[0, 0], above_ref[...]))
    top_half = top.astype(BF16)
    solved = []
    for j in range(leaves):
        back = times(basis_ref[j], top_half).astype(BF16)
        solved.append((rows_ref[j] - times(inverse_ref[j], back)).astype(BF16))
    place = lax.broadcasted_iota(jnp.int16, (rows, rows), 0) == order_ref[...].astype(jnp.int16)
    pick = jnp.where(place, BF16(1), BF16(0))
    solved = jnp.concatenate(solved, axis=0)
    size = rows // 4
    moves = []
    for k in range(4):
        part = pl.ds(k * size, size)
        out_ref[part] = times(pick[k * size : (k + 1) * size], solved).astype(BF16)
        moves.append(pltpu.make_async_copy(out_ref.at[part], out_hbm.at[part], sems.at[k]))
        moves[-1].start()
    for move in moves:
        move.wait()


def on_device(
    rhs, order, leaf_inverse, leaf_column_generator, factor_up, downward_coupling_factors
):
    leaves, leaf = leaf_inverse.shape[:2]
    rank = leaf_column_generator.shape[2]
    genes = rhs.shape[1]
    levels = factor_up.shape[1]
    last = levels - 1
    low = last - 1
    col_bits = lax.axis_size("col").bit_length() - 1
    up, down = factor_up, downward_coupling_factors
    small = (rank, genes)
    steps = [(small, BF16), (small, BF16)]

    rows, state, term, share = pl.pallas_call(
        functools.partial(leaf_kernel, low, col_bits),
        out_shape=[
            jax.ShapeDtypeStruct((leaves, leaf, genes), F32),
            jax.ShapeDtypeStruct(small, F32),
            jax.ShapeDtypeStruct(small, BF16),
            jax.ShapeDtypeStruct((4, 2) + factor_up.shape[2:], BF16),
        ],
        in_specs=[pl.BlockSpec(memory_space=pltpu.HBM)] * 6,
        out_specs=[pl.BlockSpec(memory_space=pltpu.VMEM if k == 2 else pltpu.HBM) for k in range(4)],
        scratch_shapes=[
            pltpu.VMEM(order.shape, order.dtype),
            pltpu.VMEM(rhs.shape, BF16),
            pltpu.VMEM(leaf_inverse.shape, BF16),
            pltpu.VMEM(leaf_column_generator.shape, BF16),
            pltpu.VMEM(factor_up.shape[2:], BF16),
            pltpu.VMEM((3,) + factor_up.shape[2:], BF16),
            pltpu.VMEM((leaves, leaf, genes), F32),
            pltpu.VMEM(small, F32),
            pltpu.SemaphoreType.DMA((8,)),
            pltpu.SemaphoreType.DMA((4,)),
            pltpu.SemaphoreType.DMA((leaves + 1,)),
        ],
        compiler_params=pltpu.CompilerParams(vmem_limit_bytes=56 * MIB),
    )(order, rhs, leaf_inverse, leaf_column_generator, up, down)
    term, up = lax.optimization_barrier((term, up))
    pairs = [both(term, 0, col_bits)]
    shared = among_four(share, low, col_bits)
    for level in range(1, low):
        (term,) = call(functools.partial(up_kernel, level), [(small, BF16)], 2, 4 * MIB)(pairs[-1], up)
        pairs.append(both(term, level, col_bits))
    (term,) = call(functools.partial(up_kernel, low), [(small, BF16)], 2, 4 * MIB)(pairs[-1], up)
    term, shared = lax.optimization_barrier((term, shared))
    terms = both(term, low, col_bits)
    (half,) = call(state_kernel, [(small, BF16)], 1, 4 * MIB)(terms)
    y, sent = call(functools.partial(top_kernel, low, col_bits), steps, 6, 8 * MIB)(
        terms, across_both(half, low, col_bits), shared, pairs[-1], up, down
    )
    for level in range(low - 1, 0, -1):
        y, sent = call(functools.partial(down_kernel, level, col_bits), steps, 5, 6 * MIB)(
            both(sent, level, col_bits), pairs[level - 1], y, up, down
        )
    (solved,) = pl.pallas_call(
        functools.partial(last_kernel, col_bits),
        out_shape=[jax.ShapeDtypeStruct(rhs.shape, BF16)],
        in_specs=[pl.BlockSpec(memory_space=pltpu.VMEM)] * 8,
        out_specs=[pl.BlockSpec(memory_space=pltpu.HBM)],
        scratch_shapes=[pltpu.VMEM(rhs.shape, BF16), pltpu.SemaphoreType.DMA((4,))],
        compiler_params=pltpu.CompilerParams(vmem_limit_bytes=24 * MIB),
    )(order, both(sent, 0, col_bits), state, y, up, leaf_inverse, leaf_column_generator, rows)
    return solved


def solution(mesh):
    in_specs = (
        P(("row", "col"), None),
        P(("row", "col"), None),
        P(("row", "col"), None, None),
        P(("row", "col"), None, None),
        P(("row", "col"), None, None, None),
        P(("row", "col"), None, None, None),
    )
    out_specs = P(("row", "col"), None)

    return jax.shard_map(on_device, mesh=mesh, in_specs=in_specs, out_specs=out_specs, check_vma=False)
```
